32 devices in a mesh: section: 2 (over y), design: 8 (over z, x), batch: 2 (over core).
Axes of the slice: x: 2, y: 2, z: 4, core: 2. Of those that a mesh axis runs over, the one named last changes fastest.
Arguments:
- samples: float32 [64, 4096], replicated, may hold values from -6 to 6
- order: int32 [4096], P('batch'), may hold values from 0 to 4095, each once
- design_points: bfloat16 [2, 64, 16384], P('section', None, 'design'), may hold values from -6 to 6
- weights: bfloat16 [2, 64, 16384], P('section', None, 'design'), may hold values from -2 to 2
- length_sq: float32 [2, 64], replicated, may hold values from 8 to 128
Outputs:
- moments: float32 [2, 4, 64, 1024], P('section', None, None, ('batch', 'design'))
The draws below stay inside these ranges and needn't reach their ends.
Inputs may be any that keep to these rules, and one draw needn't show every extreme that they name: `order`: each sample index appears exactly once.
All inputs are finite; a program needn't handle non-finite values.
Results may differ from the reference program's by a relative error of at most 0.0037.
Values may be sent and summed in bfloat16 or wider, within the bound.
A program may use at most 64 MiB of HBM per device.

```python
import math
import jax
import jax.numpy as jnp
from jax import lax

FEAT = 64
OUT1 = 32
DES_DEV = 2048
MICRO = 512
SAMPLES = 4096
NDES = 16384
NMB = 4
N_DESIGN = 8
N_BATCH = 2


def steps_of(stream_key, extent, shards, smallest, largest):
    level = 1.0
    for axis_at, parts in shards:
        heights = jax.random.uniform(jax.random.fold_in(jax.random.fold_in(stream_key, 6), axis_at), (parts,), jnp.float32, smallest / len(shards), largest / len(shards))
        level = level * jnp.repeat(jnp.exp(heights), extent[axis_at] // parts).reshape((-1,) + (1,) * (len(extent) - 1 - axis_at))
    return level


def gaussian(own_key, extent, spread, most, shards=(), kind=jnp.bfloat16):
    loudness = steps_of(own_key, extent, shards, -0.22, 0.18) if shards else 1.0
    values = jax.random.normal(own_key, extent, jnp.float32) * spread * loudness
    return jnp.minimum(jnp.maximum(values, -most), most).astype(kind)


def setup_inputs(seed: int = 0) -> dict:
    splits = jax.random.split(jax.random.key(seed), 6)
    return {
        "samples": gaussian(splits[0], (FEAT, SAMPLES), 1.0, 6.0, (), jnp.float32),
        "order": jax.random.permutation(splits[1], SAMPLES).astype(jnp.int32),
        "design_points": gaussian(splits[2], (2, FEAT, NDES), 1.0, 6.0, ((0, 2), (2, 8))),
        "weights": gaussian(splits[3], (2, FEAT, NDES), (max(1, DES_DEV * N_DESIGN // 2048)) ** -0.5, 2.0, ((0, 2), (2, 8))),
        "length_sq": jnp.clip(jnp.exp(jax.random.uniform(splits[4], (2, FEAT), jnp.float32, math.log(8.0), math.log(128.0))), 8.0, 128.0),
    }


def layer_sum(mean_in, var_in, design, weight_rows, lengths):
    denom = lengths[:, None] + 2.0 * var_in
    offset = jnp.sum(mean_in * mean_in / denom, axis=0)
    log_scale = -0.5 * jnp.sum(jnp.log(1.0 + 2.0 * var_in / lengths[:, None]), axis=0)
    scaled = (mean_in / denom).astype(jnp.bfloat16)
    inverse = (1.0 / denom).astype(jnp.bfloat16)
    feat = design.shape[0]
    blocks = design.reshape(feat, N_DESIGN, DES_DEV).transpose(1, 0, 2)
    weight_blocks = weight_rows.reshape(feat, N_DESIGN, DES_DEV).transpose(1, 0, 2)

    def step(total, pair):
        points, block_weights = pair
        wide = points.astype(jnp.float32)
        squares = (wide * wide).astype(jnp.bfloat16)
        cross = jnp.dot(scaled.T, points, preferred_element_type=jnp.float32)
        quad = jnp.dot(inverse.T, squares, preferred_element_type=jnp.float32)
        kernel = jnp.exp(log_scale[:, None] - offset[:, None] + 2.0 * cross - quad).astype(jnp.bfloat16)
        return total + jnp.dot(block_weights, kernel.T, preferred_element_type=jnp.float32), None

    start = jnp.zeros((feat, mean_in.shape[1]), jnp.float32)
    total, _ = lax.scan(step, start, (blocks, weight_blocks))
    return total


def reference(samples, order, design_points, weights, length_sq):
    feat = samples.shape[0]
    half = OUT1
    order_blocks = order.reshape(N_BATCH * NMB, MICRO)

    def one_block(indices):
        chosen = jnp.take(samples, indices.astype(jnp.int32), axis=1)
        zeros_var = jnp.zeros((feat, MICRO), jnp.float32)
        land = layer_sum(chosen, zeros_var, design_points[0], weights[0], length_sq[0])
        mean_one = land[:half]
        var_one = jax.nn.softplus(land[half:])
        first = jnp.concatenate([mean_one, var_one], axis=0)
        mean_two = jnp.concatenate([mean_one, chosen[half:]], axis=0)
        var_two = jnp.concatenate([var_one, jnp.zeros((feat - half, MICRO), jnp.float32)], axis=0)
        atmos = layer_sum(mean_two, var_two, design_points[1], weights[1], length_sq[1])
        return jnp.stack([first, atmos], axis=0)

    result = lax.map(one_block, order_blocks)
    result = result.reshape(N_BATCH, NMB, 2, feat, MICRO).transpose(2, 1, 3, 0, 4)
    return result.reshape(2, NMB, feat, N_BATCH * MICRO)
```

```python
import functools

import jax
import jax.numpy as jnp
from jax import lax
from jax.experimental import pallas as pl
from jax.experimental.pallas import tpu as pltpu
from jax.sharding import PartitionSpec as P

MICRO = 512
TILE = 256
MESH = pl.DeviceIdType.MESH


def gather_kernel(order_ref, samples_ref, out_ref, rows_ref, picked_ref):
    total = samples_ref.shape[1]
    for start in range(0, total, MICRO):
        rows_ref[start : start + MICRO, :] = samples_ref[:, start : start + MICRO].T
    group = 32

    def pick(step, carry):
        base = pl.multiple_of(step * group, group)
        for k in range(group):
            picked_ref[pl.ds(base + k, 1), :] = rows_ref[pl.ds(order_ref[base + k], 1), :]
        return carry

    lax.fori_loop(0, order_ref.shape[0] // group, pick, 0)
    for turn in range(out_ref.shape[0]):
        out_ref[turn] = picked_ref[turn * MICRO : (turn + 1) * MICRO, :].T


def gather(samples, order):
    feat, total = samples.shape
    return pl.pallas_call(
        gather_kernel,
        out_shape=jax.ShapeDtypeStruct((order.shape[0] // MICRO, feat, MICRO), jnp.float32),
        in_specs=[
            pl.BlockSpec(memory_space=pltpu.SMEM),
            pl.BlockSpec(memory_space=pltpu.VMEM),
        ],
        out_specs=pl.BlockSpec(memory_space=pltpu.VMEM),
        scratch_shapes=[
            pltpu.VMEM((total, feat), jnp.float32),
            pltpu.VMEM((order.shape[0], feat), jnp.float32),
        ],
    )(order, samples)


def softplus(x):
    return jnp.maximum(x, 0.0) + jnp.log1p(jnp.exp(-jnp.abs(x)))


def main_kernel(
    sizes,
    chosen_ref,
    points_ref,
    weights_ref,
    length_ref,
    out_ref,
    sides_ref,
    mean_ref,
    var_ref,
    out_blocks,
    in_blocks,
    land_block,
    land_in,
    sum_sent,
    sum_came,
    land_sent,
    land_came,
):
    devices, count, feat, half, share = sizes
    me = lax.axis_index("design")
    section = lax.axis_index("section")
    is_land = section == 0
    runs = points_ref.shape[2]

    barrier = pltpu.get_barrier_semaphore()

    def greet_peer(step, carry):
        peer = lax.rem(me + step, devices)
        pl.semaphore_signal(barrier, inc=1, device_id={"design": peer}, device_id_type=MESH)
        return carry

    def greet_other(peer, carry):
        pl.semaphore_signal(
            barrier, inc=1, device_id={"section": 1 - section, "design": peer}, device_id_type=MESH
        )
        return carry

    lax.fori_loop(1, devices, greet_peer, 0)
    lax.fori_loop(0, devices, greet_other, 0)

    for start in range(0, runs, MICRO):
        wide = points_ref[0, :, start : start + MICRO].astype(jnp.float32)
        squares = (wide * wide).astype(jnp.bfloat16).astype(jnp.float32)
        both = jnp.concatenate([wide, squares], axis=0)
        sides_ref[start : start + MICRO, :] = both.T.astype(jnp.bfloat16)

    row = jnp.where(is_land, length_ref[0:1, :], length_ref[1:2, :])
    spread = jnp.broadcast_to(row, (feat, feat))
    on_diagonal = lax.broadcasted_iota(jnp.int32, (feat, feat), 0) == lax.broadcasted_iota(
        jnp.int32, (feat, feat), 1
    )
    lengths = jnp.sum(jnp.where(on_diagonal, spread, 0.0), axis=1, keepdims=True)
    var_ref[...] = jnp.zeros_like(var_ref)

    def finish(turn):
        pltpu.make_async_copy(
            in_blocks.at[turn, pl.ds(0, devices - 1)],
            in_blocks.at[turn, pl.ds(0, devices - 1)],
            sum_came.at[turn],
        ).wait()
        total = in_blocks[turn, 0].astype(jnp.float32)
        for peer in range(1, devices):
            total = total + in_blocks[turn, peer].astype(jnp.float32)
        lane = lax.broadcasted_iota(jnp.int32, total.shape, 1)
        total = jnp.where(jnp.logical_and(is_land, lane >= share), softplus(total), total)

        @pl.when(is_land)
        def _():
            land_block[turn] = total

            def pass_on(peer, carry):
                pltpu.make_async_remote_copy(
                    src_ref=land_block.at[turn],
                    dst_ref=land_in.at[turn, me],
                    send_sem=land_sent.at[turn],
                    recv_sem=land_came.at[turn],
                    device_id={"section": 1, "design": peer},
                    device_id_type=MESH,
                ).start()
                return carry

            lax.fori_loop(0, devices, pass_on, 0)

        out_ref[0, turn, :half, :] = total[:, :share]
        out_ref[0, turn, half:, :] = total[:, share:]

    def step(turn, carry):
        @pl.when(is_land)
        def _():
            mean_ref[...] = chosen_ref[turn]

        @pl.when(jnp.logical_not(is_land))
        def _():
            pltpu.make_async_copy(land_in.at[turn], land_in.at[turn], land_came.at[turn]).wait()
            blocks = [land_in[turn, peer] for peer in range(devices)]
            mean_ref[:half, :] = jnp.concatenate([b[:, :share] for b in blocks], axis=1)
            mean_ref[half:, :] = chosen_ref[turn, half:, :]
            var_ref[:half, :] = jnp.concatenate([b[:, share:] for b in blocks], axis=1)

        mean = mean_ref[...]
        var = var_ref[...]
        inverse = 1.0 / (lengths + 2.0 * var)
        scaled = mean * inverse
        bias = -jnp.sum(mean * scaled, axis=0, keepdims=True) - 0.5 * jnp.sum(
            jnp.log(1.0 + 2.0 * var / lengths), axis=0, keepdims=True
        )
        factors = jnp.concatenate(
            [2.0 * scaled.astype(jnp.bfloat16).astype(jnp.float32), -inverse], axis=0
        ).astype(jnp.bfloat16)
        total = jnp.zeros((feat, MICRO), jnp.float32)
        for start in range(0, runs, TILE):
            exponent = jnp.dot(
                sides_ref[start : start + TILE, :], factors, preferred_element_type=jnp.float32
            )
            kernel = jnp.exp(exponent + bias).astype(jnp.bfloat16)
            total = total + jnp.dot(
                weights_ref[0, :, start : start + TILE], kernel, preferred_element_type=jnp.float32
            )
        for peer in range(devices):
            piece = total[:, peer * share : (peer + 1) * share]
            out_blocks[turn, peer] = jnp.concatenate([piece[:half], piece[half:]], axis=1).astype(
                out_blocks.dtype
            )
        in_blocks[turn, me] = out_blocks[turn, me]

        @pl.when(turn == 0)
        def _():
            pl.semaphore_wait(barrier, 2 * devices - 1)

        def hand_over(distance, carry):
            peer = lax.rem(me + distance, devices)
            pltpu.make_async_remote_copy(
                src_ref=out_blocks.at[turn, peer],
                dst_ref=in_blocks.at[turn, me],
                send_sem=sum_sent.at[turn],
                recv_sem=sum_came.at[turn],
                device_id={"design": peer},
                device_id_type=MESH,
            ).start()
            return carry

        lax.fori_loop(1, devices, hand_over, 0)

        @pl.when(turn > 0)
        def _():
            finish(turn - 1)

        return carry

    lax.fori_loop(0, count, step, 0)
    finish(count - 1)

    def drain(turn, carry):
        pltpu.make_async_copy(
            out_blocks.at[turn, pl.ds(0, devices - 1)],
            out_blocks.at[turn, pl.ds(0, devices - 1)],
            sum_sent.at[turn],
        ).wait()

        @pl.when(is_land)
        def _():
            pltpu.make_async_copy(land_in.at[turn], land_in.at[turn], land_sent.at[turn]).wait()

        return carry

    lax.fori_loop(0, count, drain, 0)


def shards(samples, order, design_points, weights, length_sq):
    feat = samples.shape[0]
    runs = design_points.shape[2]
    half = feat // 2
    count = order.shape[0] // MICRO
    devices = lax.axis_size("design")
    share = MICRO // devices
    chosen = gather(samples, order)
    vmem = pl.BlockSpec(memory_space=pltpu.VMEM)
    return pl.pallas_call(
        functools.partial(main_kernel, (devices, count, feat, half, share)),
        out_shape=jax.ShapeDtypeStruct((1, count, feat, share), jnp.float32),
        in_specs=[vmem] * 4,
        out_specs=vmem,
        scratch_shapes=[
            pltpu.VMEM((runs, 2 * feat), jnp.bfloat16),
            pltpu.VMEM((feat, MICRO), jnp.float32),
            pltpu.VMEM((feat, MICRO), jnp.float32),
            pltpu.VMEM((count, devices, half, 2 * share), jnp.bfloat16),
            pltpu.VMEM((count, devices, half, 2 * share), jnp.bfloat16),
            pltpu.VMEM((count, half, 2 * share), jnp.float32),
            pltpu.VMEM((count, devices, half, 2 * share), jnp.float32),
            pltpu.SemaphoreType.DMA((count,)),
            pltpu.SemaphoreType.DMA((count,)),
            pltpu.SemaphoreType.DMA((count,)),
            pltpu.SemaphoreType.DMA((count,)),
        ],
        compiler_params=pltpu.CompilerParams(collective_id=0, has_side_effects=True),
    )(chosen, design_points, weights, length_sq)


def solution(mesh):
    placed = (P(), P("batch"), P("section", None, "design"), P("section", None, "design"), P())
    return jax.shard_map(
        shards,
        mesh=mesh,
        in_specs=placed,
        out_specs=P("section", None, None, ("batch", "design")),
        check_vma=False,
    )
```

```python
import functools

import jax
import jax.numpy as jnp
from jax import lax
from jax.experimental import pallas as pl
from jax.experimental.pallas import tpu as pltpu
from jax.sharding import PartitionSpec as P

MICRO = 512
TILE = 256
MESH = pl.DeviceIdType.MESH


def softplus(x):
    return jnp.maximum(x, 0.0) + jnp.log1p(jnp.exp(-jnp.abs(x)))


def main_kernel(
    sizes,
    order_ref,
    samples_ref,
    points_ref,
    weights_ref,
    length_ref,
    out_ref,
    rows_ref,
    picked_ref,
    sides_ref,
    mean_ref,
    var_ref,
    out_blocks,
    in_blocks,
    land_block,
    land_in,
    sum_sent,
    sum_came,
    land_sent,
    land_came,
):
    devices, count, feat, half, share = sizes
    me = lax.axis_index("design")
    section = lax.axis_index("section")
    is_land = section == 0
    runs = points_ref.shape[2]

    barrier = pltpu.get_barrier_semaphore()

    def greet_peer(step, carry):
        peer = lax.rem(me + step, devices)
        pl.semaphore_signal(barrier, inc=1, device_id={"design": peer}, device_id_type=MESH)
        return carry

    def greet_other(peer, carry):
        pl.semaphore_signal(
            barrier, inc=1, device_id={"section": 1 - section, "design": peer}, device_id_type=MESH
        )
        return carry

    lax.fori_loop(1, devices, greet_peer, 0)
    lax.fori_loop(0, devices, greet_other, 0)

    for start in range(0, samples_ref.shape[1], MICRO):
        rows_ref[start : start + MICRO, :] = samples_ref[:, start : start + MICRO].T

    def pick(source, slot, first, number):
        for at in range(first, first + number):
            index = order_ref[source * MICRO + at]
            picked_ref[slot, at : at + 1, :] = rows_ref[pl.ds(index, 1), :]

    pick(0, 0, 0, MICRO)

    for start in range(0, runs, MICRO):
        wide = points_ref[0, :, start : start + MICRO].astype(jnp.float32)
        squares = (wide * wide).astype(jnp.bfloat16).astype(jnp.float32)
        both = jnp.concatenate([wide, squares], axis=0)
        sides_ref[start : start + MICRO, :] = both.T.astype(jnp.bfloat16)

    row = jnp.where(is_land, length_ref[0:1, :], length_ref[1:2, :])
    spread = jnp.broadcast_to(row, (feat, feat))
    on_diagonal = lax.broadcasted_iota(jnp.int32, (feat, feat), 0) == lax.broadcasted_iota(
        jnp.int32, (feat, feat), 1
    )
    lengths = jnp.sum(jnp.where(on_diagonal, spread, 0.0), axis=1, keepdims=True)
    var_ref[...] = jnp.zeros_like(var_ref)

    def finish(turn):
        pltpu.make_async_copy(
            in_blocks.at[turn, pl.ds(0, devices - 1)],
            in_blocks.at[turn, pl.ds(0, devices - 1)],
            sum_came.at[turn],
        ).wait()
        total = in_blocks[turn, 0].astype(jnp.float32)
        for peer in range(1, devices):
            total = total + in_blocks[turn, peer].astype(jnp.float32)
        lane = lax.broadcasted_iota(jnp.int32, total.shape, 1)
        total = jnp.where(jnp.logical_and(is_land, lane >= share), softplus(total), total)

        @pl.when(is_land)
        def _():
            land_block[turn] = total

            def pass_on(peer, carry):
                pltpu.make_async_remote_copy(
                    src_ref=land_block.at[turn],
                    dst_ref=land_in.at[turn, me],
                    send_sem=land_sent.at[turn],
                    recv_sem=land_came.at[turn],
                    device_id={"section": 1, "design": peer},
                    device_id_type=MESH,
                ).start()
                return carry

            lax.fori_loop(0, devices, pass_on, 0)

        out_ref[0, turn, :half, :] = total[:, :share]
        out_ref[0, turn, half:, :] = total[:, share:]

    def step(turn, carry):
        slot = lax.rem(turn, 2)
        chosen = picked_ref[slot].T

        @pl.when(is_land)
        def _():
            mean_ref[...] = chosen

        @pl.when(jnp.logical_not(is_land))
        def _():
            pltpu.make_async_copy(land_in.at[turn], land_in.at[turn], land_came.at[turn]).wait()
            blocks = [land_in[turn, peer] for peer in range(devices)]
            mean_ref[:half, :] = jnp.concatenate([b[:, :share] for b in blocks], axis=1)
            mean_ref[half:, :] = chosen[half:, :]
            var_ref[:half, :] = jnp.concatenate([b[:, share:] for b in blocks], axis=1)

        mean = mean_ref[...]
        var = var_ref[...]
        inverse = 1.0 / (lengths + 2.0 * var)
        scaled = mean * inverse
        bias = -jnp.sum(mean * scaled, axis=0, keepdims=True) - 0.5 * jnp.sum(
            jnp.log(1.0 + 2.0 * var / lengths), axis=0, keepdims=True
        )
        factors = jnp.concatenate(
            [2.0 * scaled.astype(jnp.bfloat16).astype(jnp.float32), -inverse], axis=0
        ).astype(jnp.bfloat16)
        total = jnp.zeros((feat, MICRO), jnp.float32)
        following = jnp.minimum(turn + 1, count - 1)
        portion = MICRO * TILE // runs
        for start in range(0, runs, TILE):
            pick(following, 1 - slot, start // TILE * portion, portion)
            exponent = jnp.dot(
                sides_ref[start : start + TILE, :], factors, preferred_element_type=jnp.float32
            )
            kernel = jnp.exp(exponent + bias).astype(jnp.bfloat16)
            total = total + jnp.dot(
                weights_ref[0, :, start : start + TILE], kernel, preferred_element_type=jnp.float32
            )
        for peer in range(devices):
            piece = total[:, peer * share : (peer + 1) * share]
            out_blocks[turn, peer] = jnp.concatenate([piece[:half], piece[half:]], axis=1).astype(
                out_blocks.dtype
            )
        in_blocks[turn, me] = out_blocks[turn, me]

        @pl.when(turn == 0)
        def _():
            pl.semaphore_wait(barrier, 2 * devices - 1)

        def hand_over(distance, carry):
            peer = lax.rem(me + distance, devices)
            pltpu.make_async_remote_copy(
                src_ref=out_blocks.at[turn, peer],
                dst_ref=in_blocks.at[turn, me],
                send_sem=sum_sent.at[turn],
                recv_sem=sum_came.at[turn],
                device_id={"design": peer},
                device_id_type=MESH,
            ).start()
            return carry

        lax.fori_loop(1, devices, hand_over, 0)

        @pl.when(turn > 0)
        def _():
            finish(turn - 1)

        return carry

    lax.fori_loop(0, count, step, 0)
    finish(count - 1)

    def drain(turn, carry):
        pltpu.make_async_copy(
            out_blocks.at[turn, pl.ds(0, devices - 1)],
            out_blocks.at[turn, pl.ds(0, devices - 1)],
            sum_sent.at[turn],
        ).wait()

        @pl.when(is_land)
        def _():
            pltpu.make_async_copy(land_in.at[turn], land_in.at[turn], land_sent.at[turn]).wait()

        return carry

    lax.fori_loop(0, count, drain, 0)


def shards(samples, order, design_points, weights, length_sq):
    feat = samples.shape[0]
    runs = design_points.shape[2]
    half = feat // 2
    count = order.shape[0] // MICRO
    devices = lax.axis_size("design")
    share = MICRO // devices
    vmem = pl.BlockSpec(memory_space=pltpu.VMEM)
    return pl.pallas_call(
        functools.partial(main_kernel, (devices, count, feat, half, share)),
        out_shape=jax.ShapeDtypeStruct((1, count, feat, share), jnp.float32),
        in_specs=[pl.BlockSpec(memory_space=pltpu.SMEM)] + [vmem] * 4,
        out_specs=vmem,
        scratch_shapes=[
            pltpu.VMEM((samples.shape[1], feat), jnp.float32),
            pltpu.VMEM((2, MICRO, feat), jnp.float32),
            pltpu.VMEM((runs, 2 * feat), jnp.bfloat16),
            pltpu.VMEM((feat, MICRO), jnp.float32),
            pltpu.VMEM((feat, MICRO), jnp.float32),
            pltpu.VMEM((count, devices, half, 2 * share), jnp.bfloat16),
            pltpu.VMEM((count, devices, half, 2 * share), jnp.bfloat16),
            pltpu.VMEM((count, half, 2 * share), jnp.float32),
            pltpu.VMEM((count, devices, half, 2 * share), jnp.float32),
            pltpu.SemaphoreType.DMA((count,)),
            pltpu.SemaphoreType.DMA((count,)),
            pltpu.SemaphoreType.DMA((count,)),
            pltpu.SemaphoreType.DMA((count,)),
        ],
        compiler_params=pltpu.CompilerParams(collective_id=0, has_side_effects=True),
    )(order, samples, design_points, weights, length_sq)


def solution(mesh):
    placed = (P(), P("batch"), P("section", None, "design"), P("section", None, "design"), P())
    return jax.shard_map(
        shards,
        mesh=mesh,
        in_specs=placed,
        out_specs=P("section", None, None, ("batch", "design")),
        check_vma=False,
    )
```
